32 devices in a mesh: seq: 8 (over z, y), head: 4 (over x, core).
Axes of the slice: x: 2, y: 2, z: 4, core: 2. Of those that a mesh axis runs over, the one named last changes fastest.
Arguments:
- q_latent: bfloat16 [1024, 32, 576], P('seq', 'head'), may hold values from -6 to 6
- kv_latent: bfloat16 [1024, 576], P('seq'), may hold values from -6 to 6
- normalizer: float32 [1024, 32], P('seq', 'head'), may hold values from 3 to 8
- q_index: bfloat16 [1024, 16, 128], P('seq', 'head'), may hold values from -0.5 to 0.5
- k_index: bfloat16 [1024, 128], P('seq'), may hold values from -6 to 6
- index_weight: float32 [1024, 16], P('seq', 'head'), may hold values from -6 to 6
- span_pos: int32 [16], replicated, may hold values from 0 to 15, each once
Outputs:
- grad_query: float32 [1024, 16, 128], P('seq', 'head')
- grad_weight: float32 [1024, 16], P('seq', 'head')
- grad_key: float32 [1024, 128], P('seq')
The draws below stay inside these ranges and needn't reach their ends.
Inputs may be any that keep to these rules, and one draw needn't show every extreme that they name: `span_pos`: each span position appears exactly once.
All inputs are finite; a program needn't handle non-finite values.
Results may differ from the reference program's by a relative error of at most 0.0085.
Values may be sent and summed in bfloat16 or wider, within the bound.
A program may use at most 64 MiB of HBM per device.

```python
import jax
import jax.numpy as jnp
from jax import lax

LATENT = 576
IDIM = 128
HEAD_DEV = 8
Q_DEV = 128
HEADS = 32
IHEADS = 16
SEQ = 1024
SPAN = 64
SPANS = 16
N_SEQ = 8


def draw_index_weight(key, part):
    key_one = jax.random.fold_in(jax.random.fold_in(key, 17), 0)
    values = jnp.clip(jax.random.normal(key_one, (SEQ, IHEADS), jnp.float32), -6.0, 6.0)
    return values.astype(jnp.float32)


def level_of(own_key, dims, pieces, low, largest):
    loudness = 1.0
    for dim, shards_of in pieces:
        draws = jax.random.uniform(jax.random.fold_in(jax.random.fold_in(own_key, 6), dim), (shards_of,), jnp.float32, low / len(pieces), largest / len(pieces))
        loudness = loudness * jnp.repeat(jnp.exp(draws), dims[dim] // shards_of).reshape((-1,) + (1,) * (len(dims) - 1 - dim))
    return loudness


def normal_values(own_key, dims, spread, most, shards=(), held_as=jnp.bfloat16):
    gain = level_of(own_key, dims, shards, -0.22, 0.18) if shards else 1.0
    entries = jax.random.normal(own_key, dims, jnp.float32) * spread * gain
    return jnp.minimum(jnp.maximum(entries, -most), most).astype(held_as)


def setup_inputs(seed: int = 0) -> dict:
    seeds = jax.random.split(jax.random.key(seed), 8)
    return {
        "q_latent": normal_values(seeds[0], (SEQ, HEADS, LATENT), 1.0, 6.0, ((0, 8), (1, 4))),
        "kv_latent": normal_values(seeds[1], (SEQ, LATENT), 1.0, 6.0, ((0, 8),)),
        "normalizer": jnp.clip(3.0 + 5.0 * jax.random.uniform(seeds[2], (SEQ, HEADS), jnp.float32) ** level_of(seeds[2], (SEQ, HEADS), ((0, 8), (1, 4)), -0.2, 0.2), 3.0, 8.0),
        "q_index": normal_values(seeds[3], (SEQ, IHEADS, IDIM), IDIM ** -0.5, 0.5, ((0, 8), (1, 4))),
        "k_index": normal_values(seeds[4], (SEQ, IDIM), 1.0, 6.0, ((0, 8),)),
        "index_weight": draw_index_weight(jax.random.fold_in(seeds[7], 71), 0),
        "span_pos": jax.random.permutation(seeds[6], SPANS).astype(jnp.int32),
    }


softmax_scale = 192.0 ** -0.5


def positions(span_pos):
    offsets = jnp.arange(SPAN, dtype=jnp.int32)
    return (span_pos[:, None] * SPAN + offsets[None, :]).reshape(-1).astype(jnp.int32)


def reference(q_latent, kv_latent, normalizer, q_index, k_index, index_weight, span_pos):
    token_pos = positions(span_pos)
    latent_keys = kv_latent.astype(jnp.float32)
    index_keys = k_index.astype(jnp.float32)
    groups = HEADS // HEAD_DEV

    def one_block(key_grad, block_index):
        first_row = (block_index * Q_DEV).astype(jnp.int32)
        queries = lax.dynamic_slice_in_dim(q_latent, first_row, Q_DEV, 0).astype(jnp.float32)
        stored = lax.dynamic_slice_in_dim(normalizer, first_row, Q_DEV, 0)
        index_queries = lax.dynamic_slice_in_dim(q_index, first_row, Q_DEV, 0).astype(jnp.float32)
        weights = lax.dynamic_slice_in_dim(index_weight, first_row, Q_DEV, 0)
        query_pos = lax.dynamic_slice_in_dim(token_pos, first_row, Q_DEV, 0)
        visible = token_pos[None, :] <= query_pos[:, None]
        grouped_q = queries.reshape(Q_DEV, groups, HEAD_DEV, LATENT).transpose(1, 0, 2, 3)
        grouped_l = stored.reshape(Q_DEV, groups, HEAD_DEV).transpose(1, 2, 0)

        def one_group(total, inputs):
            group_q, group_l = inputs
            scores = jnp.einsum('qhl,kl->hqk', group_q, latent_keys, precision=lax.Precision.HIGHEST) * softmax_scale
            attention = jnp.where(visible[None], jnp.exp(scores - group_l[:, :, None]), 0.0)
            partial_sum = jnp.sum(attention, axis=0)
            rounded = lax.optimization_barrier(partial_sum.astype(jnp.bfloat16)).astype(jnp.float32)
            return total + rounded, None

        target_raw, _ = lax.scan(one_group, jnp.zeros((Q_DEV, SEQ), jnp.float32), (grouped_q, grouped_l))
        target = target_raw / jnp.sum(target_raw, axis=1)[:, None]
        index_score = jnp.einsum('qhd,kd->hqk', index_queries, index_keys, precision=lax.Precision.HIGHEST)
        rectified = jnp.maximum(index_score, 0.0)
        logit = jnp.sum(weights.T[:, :, None] * rectified, axis=0)
        row_peak = jnp.max(jnp.where(visible, logit, -jnp.inf), axis=1)
        expo = jnp.where(visible, jnp.exp(logit - row_peak[:, None]), 0.0)
        prob = expo / jnp.sum(expo, axis=1)[:, None]
        delta = lax.optimization_barrier((prob - target).astype(jnp.bfloat16)).astype(jnp.float32)
        grad_weight = jnp.sum(delta[None] * rectified, axis=2).T
        delta_index = jnp.where(index_score > 0, delta[None] * weights.T[:, :, None], 0.0)
        delta_index = lax.optimization_barrier(delta_index.astype(jnp.bfloat16)).astype(jnp.float32)
        grad_query = jnp.einsum('hqk,kd->qhd', delta_index, index_keys, precision=lax.Precision.HIGHEST)
        key_grad = key_grad + jnp.einsum('hqk,qhd->kd', delta_index, index_queries, precision=lax.Precision.HIGHEST)
        return key_grad, (grad_query, grad_weight)

    key_grad, (grad_query, grad_weight) = lax.scan(one_block, jnp.zeros((SEQ, IDIM), jnp.float32), jnp.arange(N_SEQ, dtype=jnp.int32))
    return grad_query.reshape(SEQ, IHEADS, IDIM), grad_weight.reshape(SEQ, IHEADS), key_grad
```

```python
import functools

import jax
import jax.numpy as jnp
from jax import lax
from jax.experimental import pallas as pl
from jax.experimental.pallas import tpu as pltpu
from jax.sharding import PartitionSpec as P

MESH = pl.DeviceIdType.MESH
F32 = jnp.float32
BF16 = jnp.bfloat16
softmax_scale = 192.0 ** (-0.5)


def kernel(
    n, m, heads, iheads, span, pieces,
    q_ref, kv_ref, norm_ref, qi_ref, ki_ref, w_ref, span_ref,
    gq_ref, gw_ref, gk_ref,
    kvbuf, kibuf, qraw, qrows, normb, attn, wall, wcol, wb, qin, qall, qallt, iscore, lbuf, tbuf, trecv,
    part, gwacc, gqbuf, gqrecv, gwbuf, gwrecv, gkbuf, gkpair, gksum, gkrecv, hbuf,
    q_sem, ring_send, ring_recv, core_send, core_recv, qi_send, qi_recv, w_send, w_recv, t_send, t_recv,
    gq_send, gq_recv, gw_send, gw_recv, gp_send, gp_recv, gk_send, gk_recv, h_send, h_recv,
):
    s = lax.axis_index("seq")
    h = lax.axis_index("head")
    rows = kv_ref.shape[2]
    half = rows // 2
    latent = 2 * kv_ref.shape[1]
    depth = kv_ref.shape[1] // pieces
    tokens = rows // m
    chunk = tokens * iheads
    all_heads = m * iheads
    idim = ki_ref.shape[2]
    c = h % 2
    other = 1 - c
    partner = h + 1 - 2 * c
    near = n // 2

    def seq_at(pos):
        upper = pos // near
        return upper * (2 * (n - 1 - pos) + 1) + (1 - upper) * 2 * pos

    column = s % 2
    place = column * (n - 1 - s // 2) + (1 - column) * (s // 2)

    def seq_off(off):
        return seq_at((place + off + n) % n)

    loads = [pltpu.make_async_copy(q_ref.at[g], qraw.at[g], q_sem.at[g]) for g in range(heads)]
    for load in loads:
        load.start()
    wall[h, :, :] = jnp.concatenate([w_ref[...], jnp.zeros((8 - iheads, rows), F32)], axis=0)
    barrier = pltpu.get_barrier_semaphore()
    for d in range(1, n):
        pl.semaphore_signal(barrier, inc=1, device_id=((s + d) % n, h), device_id_type=MESH)
    for d in range(1, m):
        pl.semaphore_signal(barrier, inc=1, device_id=(s, (h + d) % m), device_id_type=MESH)
    pl.semaphore_wait(barrier, n - 1 + m - 1)

    forward = n // 2
    backward = n - 1 - forward
    offsets = {0: 0}
    for k in range(1, forward + 1):
        offsets[k] = -k
    for k in range(1, backward + 1):
        offsets[forward + k] = k
    order = [0]
    for k in range(1, forward + 1):
        order.append(k)
        if k <= backward:
            order.append(forward + k)

    pending = []

    def remote(src, dst, send, recv, device):
        copy = pltpu.make_async_remote_copy(
            src_ref=src, dst_ref=dst, send_sem=send, recv_sem=recv,
            device_id=device, device_id_type=MESH,
        )
        copy.start()
        pending.append(copy)
        return copy

    def view(kv, ki, piece):
        if piece == pieces:
            return ki
        return kv.at[pl.ds(piece * depth, depth)]

    def ring_copy(source, target, peer, piece):
        if source == 0:
            src = view(kv_ref.at[c], ki_ref.at[c], piece)
        else:
            src = view(kvbuf.at[source, c], kibuf.at[source, c], piece)
        return remote(src, view(kvbuf.at[target, c], kibuf.at[target, c], piece),
                      ring_send.at[target, piece], ring_recv.at[target, piece], (peer, h))

    def core_copy(slot, piece):
        block = view(kvbuf.at[slot, c], kibuf.at[slot, c], piece)
        return remote(block, block, core_send.at[slot, piece], core_recv.at[slot, piece], (s, partner))

    following, preceding = seq_off(1), seq_off(-1)
    ring = {}
    for piece in range(pieces + 1):
        ring[1, piece] = ring_copy(0, 1, following, piece)
        if backward:
            ring[forward + 1, piece] = ring_copy(0, forward + 1, preceding, piece)
    shared = []
    for r in range(1, m):
        peer = (h + r) % m
        shared.append(remote(qi_ref.at[pl.ds(peer * chunk, chunk)], qin.at[h],
                             qi_send.at[r - 1], qi_recv.at[r - 1], (s, peer)))
        shared.append(remote(wall.at[h], wall.at[h], w_send.at[r - 1], w_recv.at[r - 1], (s, peer)))
    kibuf[0] = ki_ref[...]
    qin[h, :, :] = qi_ref[pl.ds(h * chunk, chunk), :]

    for g in range(heads):
        normb[g * rows:(g + 1) * rows, :] = jnp.broadcast_to(norm_ref[g:g + 1, :], (rows, rows)).T
    for g, load in enumerate(loads):
        load.wait()
        qrows[g * rows:(g + 1) * rows, :] = qraw[g].T

    per_block = rows // span

    def positions(block, index):
        found = jnp.zeros(index.shape, jnp.int32)
        for t in range(per_block):
            base = span_ref[block * per_block + t]
            found = jnp.where(index // span == t, base * span + index % span, found)
        return found

    query_pos = positions(s, lax.broadcasted_iota(jnp.int32, (tokens, rows), 0) + h * tokens)

    def visible(slot):
        key_pos = positions(seq_off(offsets[slot]), lax.broadcasted_iota(jnp.int32, (tokens, rows), 1))
        return key_pos <= query_pos

    contract_last = (((1,), (1,)), ((), ()))

    def attend(slots):
        width = len(slots) * rows
        kv = jnp.concatenate(
            [(kv_ref[...] if slot == 0 else kvbuf[slot]).reshape(latent, rows) for slot in slots], axis=1
        )
        attn[:, 0:width] = jnp.dot(qrows[...], kv, preferred_element_type=F32)
        out = {}
        for i, slot in enumerate(slots):
            lanes = slice(i * rows, (i + 1) * rows)
            total = jnp.zeros((rows, rows), F32)
            for g in range(heads):
                band = slice(g * rows, (g + 1) * rows)
                total = total + jnp.exp(attn[band, lanes] * softmax_scale - normb[band, :])
            tbuf[slot] = total.astype(BF16).reshape(m, tokens, rows)
            out[slot] = [
                remote(tbuf.at[slot, (h + r) % m], trecv.at[slot, r - 1], t_send.at[slot, r - 1],
                       t_recv.at[slot, r - 1], (s, (h + r) % m))
                for r in range(1, m)
            ]
        return out

    def index(slots):
        keys = jnp.concatenate([kibuf[slot].reshape(rows, idim) for slot in slots], axis=0)
        raw_index = lax.dot_general(qall[...], keys, contract_last, preferred_element_type=F32)
        for i, slot in enumerate(slots):
            rectified = jnp.maximum(raw_index[:, i * rows:(i + 1) * rows], 0.0)
            iscore[slot] = rectified
            logit = jnp.zeros((tokens, rows), F32)
            for g in range(all_heads):
                band = slice(g * tokens, (g + 1) * tokens)
                logit = logit + wb[band, :] * rectified[band, :]
            lbuf[slot] = jnp.where(visible(slot), logit, -jnp.inf)

    second = attend([0])

    sorted_row = lax.broadcasted_iota(jnp.int32, (chunk, chunk), 0)
    stored_row = lax.broadcasted_iota(jnp.int32, (chunk, chunk), 1)
    by_head = ((sorted_row % tokens) * iheads + sorted_row // tokens == stored_row).astype(F32).astype(BF16)
    by_token = ((stored_row % tokens) * iheads + stored_row // tokens == sorted_row).astype(F32).astype(BF16)
    for copy in shared:
        copy.wait_recv()
    for r in range(m):
        qall[r * chunk:(r + 1) * chunk, :] = jnp.dot(
            by_head, qin[r], preferred_element_type=F32).astype(BF16)
    qallt[...] = qall[...].T
    wcol[...] = wall[...].reshape(m * 8, rows).T
    mine = wcol[pl.ds(h * tokens, tokens), :]
    for r in range(m):
        for g in range(iheads):
            band = slice((r * iheads + g) * tokens, (r * iheads + g + 1) * tokens)
            wb[band, :] = jnp.broadcast_to(mine[:, r * 8 + g:r * 8 + g + 1], (tokens, rows))

    waiting = [0]
    for k in range(1, forward + 1):
        arrived = [k] + ([forward + k] if k <= backward else [])
        core = {}
        for piece in range(pieces + 1):
            for slot in arrived:
                ring[slot, piece].wait_recv()
                if slot <= forward and k < forward:
                    ring[slot + 1, piece] = ring_copy(slot, slot + 1, following, piece)
                if slot > forward and k < backward:
                    ring[slot + 1, piece] = ring_copy(slot, slot + 1, preceding, piece)
                core[slot, piece] = core_copy(slot, piece)
        index(waiting)
        for slot in arrived:
            for piece in range(pieces + 1):
                core[slot, piece].wait_recv()
        second.update(attend(arrived))
        waiting = arrived
    index(waiting)

    peak = jnp.full((tokens, 1), -jnp.inf, F32)
    for slot in order:
        peak = jnp.maximum(peak, jnp.max(lbuf[slot], axis=1, keepdims=True))
    mass = jnp.zeros((tokens, 1), F32)
    for slot in order:
        expo = jnp.exp(lbuf[slot] - peak)
        lbuf[slot] = expo
        mass = mass + jnp.sum(expo, axis=1, keepdims=True)
    inv_mass = 1.0 / mass
    norm = jnp.zeros((tokens, 1), F32)
    raw = {}
    for slot in order:
        for copy in second[slot]:
            copy.wait_recv()
        total = tbuf[slot, h].astype(F32)
        for r in range(m - 1):
            total = total + trecv[slot, r].astype(F32)
        raw[slot] = jnp.where(visible(slot), total, 0.0)
        norm = norm + jnp.sum(raw[slot], axis=1, keepdims=True)
    inv_norm = 1.0 / norm
    delta = {}
    for slot in order:
        delta[slot] = (lbuf[slot] * inv_mass - raw[slot] * inv_norm).astype(BF16).astype(F32)

    incoming = []
    sums = []

    def pass_on(slot, copy):
        copy.wait_recv()
        pair = gkbuf[slot, c].astype(F32) + gkpair[slot].astype(F32)
        if slot == 0:
            return pair
        gksum[slot - 1] = pair.astype(BF16)
        incoming.append((slot, remote(
            gksum.at[slot - 1], gkrecv.at[slot - 1], gk_send.at[slot - 1],
            gk_recv.at[slot - 1], (seq_off(offsets[slot]), h))))
        return None

    own = None
    backwards = order[::-1]
    for first in range(0, n, 2):
        slots = backwards[first:first + 2]
        for g in range(all_heads):
            band = slice(g * tokens, (g + 1) * tokens)
            weight = wb[band, :]
            acc = jnp.zeros((tokens, rows), F32) if first == 0 else gwacc[band, :]
            for slot in slots:
                rectified = iscore[slot, band, :]
                acc = acc + delta[slot] * rectified
                part[band, slot * rows:(slot + 1) * rows] = jnp.where(
                    rectified > 0, delta[slot] * weight, 0.0).astype(BF16)
            gwacc[band, :] = acc
        for slot in slots:
            grad = jnp.dot(qallt[...], part[:, slot * rows:(slot + 1) * rows], preferred_element_type=F32)
            gkbuf[slot] = grad.astype(BF16).reshape(2, idim // 2, rows)
            sums.append((slot, remote(gkbuf.at[slot, other], gkpair.at[slot], gp_send.at[slot],
                                      gp_recv.at[slot], (s, partner))))
        while len(sums) > 2:
            own = pass_on(*sums.pop(0))
    while sums:
        own = pass_on(*sums.pop(0))

    keys = kibuf[...].reshape(n * rows, idim)
    returned = []
    gqbuf[...] = jnp.dot(part[...], keys, preferred_element_type=F32).astype(BF16).reshape(m, chunk, idim)
    for r in range(m):
        line = jnp.sum(gwacc[r * chunk:(r + 1) * chunk, :].T, axis=0, keepdims=True)
        gwbuf[r, :, 0:chunk] = jnp.broadcast_to(line, (8, chunk))
    for r in range(1, m):
        peer = (h + r) % m
        returned.append(remote(gqbuf.at[peer], gqrecv.at[h], gq_send.at[r - 1], gq_recv.at[r - 1], (s, peer)))
        returned.append(remote(gwbuf.at[peer], gwrecv.at[h], gw_send.at[r - 1], gw_recv.at[r - 1], (s, peer)))
    gqrecv[h, :, :] = gqbuf[h]
    gwrecv[h, :, :] = gwbuf[h]

    for slot, copy in incoming:
        copy.wait_recv()
        own = own + gkrecv[slot - 1].astype(F32)
    hbuf[h // 2, c] = own.astype(BF16)
    swaps = []
    for r in range(1, m):
        peer = (h + r) % m
        swaps.append(remote(hbuf.at[h // 2, c], hbuf.at[h // 2, c], h_send.at[r - 1],
                            h_recv.at[r - 1], (s, peer)))
    for copy in returned:
        copy.wait_recv()
    for r in range(m):
        gq_ref[r * chunk:(r + 1) * chunk, :] = jnp.dot(by_token, gqrecv[r], preferred_element_type=F32)
    lane = lax.broadcasted_iota(jnp.int32, (8, rows), 1) // tokens
    for g in range(iheads):
        line = jnp.zeros((8, rows), F32)
        for r in range(m):
            line = jnp.where(lane == r, pltpu.roll(gwrecv[r], ((r - g) * tokens) % rows, 1), line)
        gw_ref[g:g + 1, :] = line[0:1, :]
    for copy in swaps:
        copy.wait_recv()
    result = hbuf[0].reshape(idim, rows).astype(F32)
    for r in range(1, m // 2):
        result = result + hbuf[r].reshape(idim, rows).astype(F32)
    gk_ref[...] = result.T
    for copy in pending:
        copy.wait_send()


def write_out(gq_in, gw_in, gk_in, gq_ref, gw_ref, gk_ref):
    gq_ref[...] = gq_in[...]
    gw_ref[...] = gw_in[...]
    gk_ref[...] = gk_in[...]


def solution(mesh):
    n, m = mesh.shape["seq"], mesh.shape["head"]

    def on_device(q_latent, kv_latent, normalizer, q_index, k_index, index_weight, span_pos):
        rows, heads, latent = q_latent.shape
        iheads, idim = q_index.shape[1:]
        half = rows // 2
        span = rows * n // span_pos.shape[0]
        pieces = 3 if latent % 96 == 0 else 1
        V = pltpu.VMEM
        D = pltpu.SemaphoreType.DMA
        tokens = rows // m
        chunk = tokens * iheads
        scratch = [
            V((n, 2, latent // 2, rows), BF16), V((n, 2, half, idim), BF16),
            V((heads, latent, rows), BF16), V((rows * heads, latent), BF16),
            V((rows * heads, rows), F32), V((rows * heads, 2 * rows), F32),
            V((m, 8, rows), F32), V((rows, m * 8), F32), V((rows * iheads, rows), F32),
            V((m, chunk, idim), BF16), V((rows * iheads, idim), BF16), V((idim, rows * iheads), BF16),
            V((n, rows * iheads, rows), F32), V((n, tokens, rows), F32),
            V((n, m, tokens, rows), BF16), V((n, m - 1, tokens, rows), BF16),
            V((rows * iheads, n * rows), BF16), V((rows * iheads, rows), F32),
            V((m, chunk, idim), BF16), V((m, chunk, idim), BF16), V((m, 8, rows), F32), V((m, 8, rows), F32),
            V((n, 2, idim // 2, rows), BF16), V((n, idim // 2, rows), BF16), V((n - 1, idim // 2, rows), BF16),
            V((n - 1, idim // 2, rows), BF16), V((m // 2, 2, idim // 2, rows), BF16),
            D((heads,)), D((n, pieces + 1)), D((n, pieces + 1)), D((n, pieces + 1)), D((n, pieces + 1)),
            D((m - 1,)), D((m - 1,)), D((m - 1,)), D((m - 1,)), D((n, m - 1)), D((n, m - 1)),
            D((m - 1,)), D((m - 1,)), D((m - 1,)), D((m - 1,)), D((n,)), D((n,)),
            D((n - 1,)), D((n - 1,)), D((m - 1,)), D((m - 1,)),
        ]
        vmem = pl.BlockSpec(memory_space=pltpu.VMEM)
        results = pl.pallas_call(
            functools.partial(kernel, n, m, heads, iheads, span, pieces),
            out_shape=(
                jax.ShapeDtypeStruct((rows * iheads, idim), F32),
                jax.ShapeDtypeStruct((iheads, rows), F32),
                jax.ShapeDtypeStruct((rows, idim), F32),
            ),
            in_specs=[pl.BlockSpec(memory_space=pl.ANY)] + [vmem] * 5 + [pl.BlockSpec(memory_space=pltpu.SMEM)],
            out_specs=(vmem, vmem, vmem),
            scratch_shapes=scratch,
            compiler_params=pltpu.CompilerParams(
                collective_id=0, has_side_effects=True, vmem_limit_bytes=60 * 2 ** 20
            ),
        )(
            q_latent.transpose(1, 2, 0), kv_latent.T.reshape(2, latent // 2, rows),
            normalizer.T, q_index.reshape(rows * iheads, idim),
            k_index.reshape(2, half, idim), index_weight.T, span_pos,
        )
        gq, gw, gk = pl.pallas_call(
            write_out,
            out_shape=tuple(jax.ShapeDtypeStruct(x.shape, x.dtype) for x in results),
            in_specs=[vmem] * 3,
            out_specs=(vmem,) * 3,
        )(*results)
        return gq.reshape(rows, iheads, idim), gw.T, gk

    in_specs = (
        P("seq", "head", None), P("seq", None), P("seq", "head"), P("seq", "head", None),
        P("seq", None), P("seq", "head"), P(),
    )
    out_specs = (P("seq", "head", None), P("seq", "head"), P("seq", None))
    return jax.shard_map(
        on_device, mesh=mesh, in_specs=in_specs, out_specs=out_specs, check_vma=False
    )
```

```python
import functools

import jax
import jax.numpy as jnp
from jax import lax
from jax.experimental import pallas as pl
from jax.experimental.pallas import tpu as pltpu
from jax.sharding import PartitionSpec as P

MESH = pl.DeviceIdType.MESH
F32 = jnp.float32
BF16 = jnp.bfloat16
softmax_scale = 192.0 ** (-0.5)


def kernel(
    n, m, heads, iheads, span, pieces,
    q_hbm, kv_hbm, norm_hbm, qi_hbm, ki_hbm, w_hbm, span_hbm,
    gq_ref, gw_ref, gk_ref,
    kvbuf, kibuf, norm_ref, w_ref, span_ref, qraw, qrows, normb, attn, wall, wcol, wb, qin, qall, qallt, iscore, lbuf, tbuf, trecv,
    part, gwacc, gqbuf, gqrecv, gwbuf, gwrecv, gkbuf, gkpair, gksum, gkrecv, hbuf,
    q_sem, in_sem, ring_send, ring_recv, core_send, core_recv, qi_send, qi_recv, w_send, w_recv, t_send, t_recv,
    gq_send, gq_recv, gw_send, gw_recv, gp_send, gp_recv, gk_send, gk_recv, h_send, h_recv,
):
    s = lax.axis_index("seq")
    h = lax.axis_index("head")
    rows = kv_hbm.shape[2]
    half = rows // 2
    latent = 2 * kv_hbm.shape[1]
    depth = kv_hbm.shape[1] // pieces
    tokens = rows // m
    chunk = tokens * iheads
    all_heads = m * iheads
    idim = ki_hbm.shape[2]
    c = h % 2
    other = 1 - c
    partner = h + 1 - 2 * c
    near = n // 2

    def seq_at(pos):
        upper = pos // near
        return upper * (2 * (n - 1 - pos) + 1) + (1 - upper) * 2 * pos

    column = s % 2
    place = column * (n - 1 - s // 2) + (1 - column) * (s // 2)

    def seq_off(off):
        return seq_at((place + off + n) % n)

    barrier = pltpu.get_barrier_semaphore()
    beside = (1, -1) if n > 2 else (1,)
    for d in beside:
        pl.semaphore_signal(barrier, inc=1, device_id=(seq_off(d), h), device_id_type=MESH)
    for d in range(1, m):
        pl.semaphore_signal(barrier, inc=1, device_id=(s, (h + d) % m), device_id_type=MESH)
    inputs = [
        pltpu.make_async_copy(src, dst, in_sem.at[i])
        for i, (src, dst) in enumerate((
            (w_hbm, w_ref), (kv_hbm, kvbuf.at[0]), (ki_hbm, kibuf.at[0]), (norm_hbm, norm_ref),
            (qi_hbm.at[pl.ds(h * chunk, chunk)], qin.at[h]), (span_hbm, span_ref),
        ))
    ]
    loads = [pltpu.make_async_copy(q_hbm.at[g], qraw.at[g], q_sem.at[g]) for g in range(heads)]
    for load in inputs + loads:
        load.start()
    inputs[0].wait()
    wall[h, :, :] = jnp.concatenate([w_ref[...], jnp.zeros((8 - iheads, rows), F32)], axis=0)
    pl.semaphore_wait(barrier, len(beside) + m - 1)

    forward = n // 2
    backward = n - 1 - forward
    offsets = {0: 0}
    for k in range(1, forward + 1):
        offsets[k] = -k
    for k in range(1, backward + 1):
        offsets[forward + k] = k
    order = [0]
    for k in range(1, forward + 1):
        order.append(k)
        if k <= backward:
            order.append(forward + k)

    pending = []

    def remote(src, dst, send, recv, device):
        copy = pltpu.make_async_remote_copy(
            src_ref=src, dst_ref=dst, send_sem=send, recv_sem=recv,
            device_id=device, device_id_type=MESH,
        )
        copy.start()
        pending.append(copy)
        return copy

    def view(kv, ki, piece):
        if piece == pieces:
            return ki
        return kv.at[pl.ds(piece * depth, depth)]

    def ring_copy(source, target, peer, piece):
        if source == 0:
            src = view(kv_hbm.at[c], ki_hbm.at[c], piece)
        else:
            src = view(kvbuf.at[source, c], kibuf.at[source, c], piece)
        return remote(src, view(kvbuf.at[target, c], kibuf.at[target, c], piece),
                      ring_send.at[target, piece], ring_recv.at[target, piece], (peer, h))

    def core_copy(slot, piece):
        block = view(kvbuf.at[slot, c], kibuf.at[slot, c], piece)
        return remote(block, block, core_send.at[slot, piece], core_recv.at[slot, piece], (s, partner))

    following, preceding = seq_off(1), seq_off(-1)
    ring = {}
    for piece in range(pieces + 1):
        ring[1, piece] = ring_copy(0, 1, following, piece)
        if backward:
            ring[forward + 1, piece] = ring_copy(0, forward + 1, preceding, piece)
    shared = []
    for r in range(1, m):
        peer = (h + r) % m
        shared.append(remote(qi_hbm.at[pl.ds(peer * chunk, chunk)], qin.at[h],
                             qi_send.at[r - 1], qi_recv.at[r - 1], (s, peer)))
        shared.append(remote(wall.at[h], wall.at[h], w_send.at[r - 1], w_recv.at[r - 1], (s, peer)))
    for load in inputs[1:]:
        load.wait()

    for g in range(heads):
        normb[g * rows:(g + 1) * rows, :] = jnp.broadcast_to(norm_ref[g:g + 1, :], (rows, rows)).T
    for g, load in enumerate(loads):
        load.wait()
        qrows[g * rows:(g + 1) * rows, :] = qraw[g].T

    per_block = rows // span

    def positions(block, index):
        found = jnp.zeros(index.shape, jnp.int32)
        for t in range(per_block):
            base = span_ref[block * per_block + t]
            found = jnp.where(index // span == t, base * span + index % span, found)
        return found

    query_pos = positions(s, lax.broadcasted_iota(jnp.int32, (tokens, rows), 0) + h * tokens)

    def visible(slot):
        key_pos = positions(seq_off(offsets[slot]), lax.broadcasted_iota(jnp.int32, (tokens, rows), 1))
        return key_pos <= query_pos

    contract_last = (((1,), (1,)), ((), ()))

    def attend(slots):
        width = len(slots) * rows
        kv = jnp.concatenate(
            [kvbuf[slot].reshape(latent, rows) for slot in slots], axis=1
        )
        attn[:, 0:width] = jnp.dot(qrows[...], kv, preferred_element_type=F32)
        out = {}
        for i, slot in enumerate(slots):
            lanes = slice(i * rows, (i + 1) * rows)
            total = jnp.zeros((rows, rows), F32)
            for g in range(heads):
                band = slice(g * rows, (g + 1) * rows)
                total = total + jnp.exp(attn[band, lanes] * softmax_scale - normb[band, :])
            tbuf[slot] = total.astype(BF16).reshape(m, tokens, rows)
            out[slot] = [
                remote(tbuf.at[slot, (h + r) % m], trecv.at[slot, r - 1], t_send.at[slot, r - 1],
                       t_recv.at[slot, r - 1], (s, (h + r) % m))
                for r in range(1, m)
            ]
        return out

    def index(slots):
        keys = jnp.concatenate([kibuf[slot].reshape(rows, idim) for slot in slots], axis=0)
        raw_index = lax.dot_general(qall[...], keys, contract_last, preferred_element_type=F32)
        for i, slot in enumerate(slots):
            rectified = jnp.maximum(raw_index[:, i * rows:(i + 1) * rows], 0.0)
            iscore[slot] = rectified
            logit = jnp.zeros((tokens, rows), F32)
            for g in range(all_heads):
                band = slice(g * tokens, (g + 1) * tokens)
                logit = logit + wb[band, :] * rectified[band, :]
            lbuf[slot] = jnp.where(visible(slot), logit, -jnp.inf)

    second = attend([0])

    sorted_row = lax.broadcasted_iota(jnp.int32, (chunk, chunk), 0)
    stored_row = lax.broadcasted_iota(jnp.int32, (chunk, chunk), 1)
    by_head = ((sorted_row % tokens) * iheads + sorted_row // tokens == stored_row).astype(F32).astype(BF16)
    by_token = ((stored_row % tokens) * iheads + stored_row // tokens == sorted_row).astype(F32).astype(BF16)
    for copy in shared:
        copy.wait_recv()
    for r in range(m):
        qall[r * chunk:(r + 1) * chunk, :] = jnp.dot(
            by_head, qin[r], preferred_element_type=F32).astype(BF16)
    qallt[...] = qall[...].T
    wcol[...] = wall[...].reshape(m * 8, rows).T
    mine = wcol[pl.ds(h * tokens, tokens), :]
    for r in range(m):
        for g in range(iheads):
            band = slice((r * iheads + g) * tokens, (r * iheads + g + 1) * tokens)
            wb[band, :] = jnp.broadcast_to(mine[:, r * 8 + g:r * 8 + g + 1], (tokens, rows))

    waiting = [0]
    for k in range(1, forward + 1):
        arrived = [k] + ([forward + k] if k <= backward else [])
        core = {}
        for piece in range(pieces + 1):
            for slot in arrived:
                ring[slot, piece].wait_recv()
                if slot <= forward and k < forward:
                    ring[slot + 1, piece] = ring_copy(slot, slot + 1, following, piece)
                if slot > forward and k < backward:
                    ring[slot + 1, piece] = ring_copy(slot, slot + 1, preceding, piece)
                core[slot, piece] = core_copy(slot, piece)
        index(waiting)
        for slot in arrived:
            for piece in range(pieces + 1):
                core[slot, piece].wait_recv()
        second.update(attend(arrived))
        waiting = arrived
    index(waiting)

    peak = jnp.full((tokens, 1), -jnp.inf, F32)
    for slot in order:
        peak = jnp.maximum(peak, jnp.max(lbuf[slot], axis=1, keepdims=True))
    mass = jnp.zeros((tokens, 1), F32)
    for slot in order:
        expo = jnp.exp(lbuf[slot] - peak)
        lbuf[slot] = expo
        mass = mass + jnp.sum(expo, axis=1, keepdims=True)
    inv_mass = 1.0 / mass
    norm = jnp.zeros((tokens, 1), F32)
    raw = {}
    for slot in order:
        for copy in second[slot]:
            copy.wait_recv()
        total = tbuf[slot, h].astype(F32)
        for r in range(m - 1):
            total = total + trecv[slot, r].astype(F32)
        raw[slot] = jnp.where(visible(slot), total, 0.0)
        norm = norm + jnp.sum(raw[slot], axis=1, keepdims=True)
    inv_norm = 1.0 / norm
    delta = {}
    for slot in order:
        delta[slot] = (lbuf[slot] * inv_mass - raw[slot] * inv_norm).astype(BF16).astype(F32)

    incoming = []
    sums = []

    def pass_on(slot, copy):
        copy.wait_recv()
        pair = gkbuf[slot, c].astype(F32) + gkpair[slot].astype(F32)
        if slot == 0:
            return pair
        gksum[slot - 1] = pair.astype(BF16)
        incoming.append((slot, remote(
            gksum.at[slot - 1], gkrecv.at[slot - 1], gk_send.at[slot - 1],
            gk_recv.at[slot - 1], (seq_off(offsets[slot]), h))))
        return None

    own = None
    backwards = order[::-1]
    for first in range(0, n, 2):
        slots = backwards[first:first + 2]
        for g in range(all_heads):
            band = slice(g * tokens, (g + 1) * tokens)
            weight = wb[band, :]
            acc = jnp.zeros((tokens, rows), F32) if first == 0 else gwacc[band, :]
            for slot in slots:
                rectified = iscore[slot, band, :]
                acc = acc + delta[slot] * rectified
                part[band, slot * rows:(slot + 1) * rows] = jnp.where(
                    rectified > 0, delta[slot] * weight, 0.0).astype(BF16)
            gwacc[band, :] = acc
        for slot in slots:
            grad = jnp.dot(qallt[...], part[:, slot * rows:(slot + 1) * rows], preferred_element_type=F32)
            gkbuf[slot] = grad.astype(BF16).reshape(2, idim // 2, rows)
            sums.append((slot, remote(gkbuf.at[slot, other], gkpair.at[slot], gp_send.at[slot],
                                      gp_recv.at[slot], (s, partner))))
        while len(sums) > 2:
            own = pass_on(*sums.pop(0))
    while sums:
        own = pass_on(*sums.pop(0))

    keys = kibuf[...].reshape(n * rows, idim)
    returned = []
    gqbuf[...] = jnp.dot(part[...], keys, preferred_element_type=F32).astype(BF16).reshape(m, chunk, idim)
    for r in range(m):
        line = jnp.sum(gwacc[r * chunk:(r + 1) * chunk, :].T, axis=0, keepdims=True)
        gwbuf[r, :, 0:chunk] = jnp.broadcast_to(line, (8, chunk))
    for r in range(1, m):
        peer = (h + r) % m
        returned.append(remote(gqbuf.at[peer], gqrecv.at[h], gq_send.at[r - 1], gq_recv.at[r - 1], (s, peer)))
        returned.append(remote(gwbuf.at[peer], gwrecv.at[h], gw_send.at[r - 1], gw_recv.at[r - 1], (s, peer)))
    gqrecv[h, :, :] = gqbuf[h]
    gwrecv[h, :, :] = gwbuf[h]

    for slot, copy in incoming:
        copy.wait_recv()
        own = own + gkrecv[slot - 1].astype(F32)
    hbuf[h // 2, c] = own.astype(BF16)
    swaps = []
    for r in range(1, m):
        peer = (h + r) % m
        swaps.append(remote(hbuf.at[h // 2, c], hbuf.at[h // 2, c], h_send.at[r - 1],
                            h_recv.at[r - 1], (s, peer)))
    for copy in returned:
        copy.wait_recv()
    for r in range(m):
        gq_ref[r * chunk:(r + 1) * chunk, :] = jnp.dot(by_token, gqrecv[r], preferred_element_type=F32)
    lane = lax.broadcasted_iota(jnp.int32, (8, rows), 1) // tokens
    for g in range(iheads):
        line = jnp.zeros((8, rows), F32)
        for r in range(m):
            line = jnp.where(lane == r, pltpu.roll(gwrecv[r], ((r - g) * tokens) % rows, 1), line)
        gw_ref[g:g + 1, :] = line[0:1, :]
    for copy in swaps:
        copy.wait_recv()
    result = hbuf[0].reshape(idim, rows).astype(F32)
    for r in range(1, m // 2):
        result = result + hbuf[r].reshape(idim, rows).astype(F32)
    gk_ref[...] = result.T
    for copy in pending:
        copy.wait_send()


def write_out(gq_in, gw_in, gk_in, gq_ref, gw_ref, gk_ref):
    gq_ref[...] = gq_in[...]
    gw_ref[...] = gw_in[...]
    gk_ref[...] = gk_in[...]


def solution(mesh):
    n, m = mesh.shape["seq"], mesh.shape["head"]

    def on_device(q_latent, kv_latent, normalizer, q_index, k_index, index_weight, span_pos):
        rows, heads, latent = q_latent.shape
        iheads, idim = q_index.shape[1:]
        half = rows // 2
        span = rows * n // span_pos.shape[0]
        pieces = 3 if latent % 96 == 0 else 1
        V = pltpu.VMEM
        D = pltpu.SemaphoreType.DMA
        tokens = rows // m
        chunk = tokens * iheads
        scratch = [
            V((n, 2, latent // 2, rows), BF16), V((n, 2, half, idim), BF16),
            V((heads, rows), F32), V((iheads, rows), F32), pltpu.SMEM(span_pos.shape, jnp.int32),
            V((heads, latent, rows), BF16), V((rows * heads, latent), BF16),
            V((rows * heads, rows), F32), V((rows * heads, 2 * rows), F32),
            V((m, 8, rows), F32), V((rows, m * 8), F32), V((rows * iheads, rows), F32),
            V((m, chunk, idim), BF16), V((rows * iheads, idim), BF16), V((idim, rows * iheads), BF16),
            V((n, rows * iheads, rows), F32), V((n, tokens, rows), F32),
            V((n, m, tokens, rows), BF16), V((n, m - 1, tokens, rows), BF16),
            V((rows * iheads, n * rows), BF16), V((rows * iheads, rows), F32),
            V((m, chunk, idim), BF16), V((m, chunk, idim), BF16), V((m, 8, rows), F32), V((m, 8, rows), F32),
            V((n, 2, idim // 2, rows), BF16), V((n, idim // 2, rows), BF16), V((n - 1, idim // 2, rows), BF16),
            V((n - 1, idim // 2, rows), BF16), V((m // 2, 2, idim // 2, rows), BF16),
            D((heads,)), D((6,)), D((n, pieces + 1)), D((n, pieces + 1)), D((n, pieces + 1)), D((n, pieces + 1)),
            D((m - 1,)), D((m - 1,)), D((m - 1,)), D((m - 1,)), D((n, m - 1)), D((n, m - 1)),
            D((m - 1,)), D((m - 1,)), D((m - 1,)), D((m - 1,)), D((n,)), D((n,)),
            D((n - 1,)), D((n - 1,)), D((m - 1,)), D((m - 1,)),
        ]
        vmem = pl.BlockSpec(memory_space=pltpu.VMEM)
        results = pl.pallas_call(
            functools.partial(kernel, n, m, heads, iheads, span, pieces),
            out_shape=(
                jax.ShapeDtypeStruct((rows * iheads, idim), F32),
                jax.ShapeDtypeStruct((iheads, rows), F32),
                jax.ShapeDtypeStruct((rows, idim), F32),
            ),
            in_specs=[pl.BlockSpec(memory_space=pltpu.HBM)] * 7,
            out_specs=(vmem, vmem, vmem),
            scratch_shapes=scratch,
            compiler_params=pltpu.CompilerParams(
                collective_id=0, has_side_effects=True, vmem_limit_bytes=60 * 2 ** 20
            ),
        )(
            q_latent.transpose(1, 2, 0), kv_latent.T.reshape(2, latent // 2, rows),
            normalizer.T, q_index.reshape(rows * iheads, idim),
            k_index.reshape(2, half, idim), index_weight.T, span_pos,
        )
        gq, gw, gk = pl.pallas_call(
            write_out,
            out_shape=tuple(jax.ShapeDtypeStruct(x.shape, x.dtype) for x in results),
            in_specs=[vmem] * 3,
            out_specs=(vmem,) * 3,
        )(*results)
        return gq.reshape(rows, iheads, idim), gw.T, gk

    in_specs = (
        P("seq", "head", None), P("seq", None), P("seq", "head"), P("seq", "head", None),
        P("seq", None), P("seq", "head"), P(),
    )
    out_specs = (P("seq", "head", None), P("seq", "head"), P("seq", None))
    return jax.shard_map(
        on_device, mesh=mesh, in_specs=in_specs, out_specs=out_specs, check_vma=False
    )
```
